768 devices in a mesh: dp: 48 (over z, x_lo, core), pipe: 16 (over x_hi, y).
Axes of the slice: x: 4 (x_hi: 2, x_lo: 2; x = x_hi * 2 + x_lo), y: 8, z: 12, core: 2. Of those that a mesh axis runs over, the one named last changes fastest.
Arguments:
- acts_fwd: bfloat16 [16, 6144, 768], P('pipe', 'dp'), may hold values from -6 to 6
- acts_bwd: bfloat16 [16, 6144, 768], P('pipe', 'dp'), may hold values from -6 to 6
- cotangent: bfloat16 [16, 6144, 768], P('pipe', 'dp'), may hold values from -6 to 6
- lens_fwd: int32 [16, 48, 4], P('pipe', 'dp'), may hold values from 1 to 64, 128 in all within a row
- lens_bwd: int32 [16, 48, 4], P('pipe', 'dp'), may hold values from 1 to 64, 128 in all within a row
- w_proj: float32 [16, 768, 2048], P('pipe', 'dp'), may hold values from -0.21875 to 0.21875
- w_out: float32 [16, 512, 768], P('pipe', None, 'dp'), may hold values from -0.25 to 0.25
Outputs:
- next_acts: bfloat16 [16, 6144, 768], P('pipe', 'dp')
- prev_grads: bfloat16 [16, 6144, 768], P('pipe', 'dp')
- grad_proj: float32 [16, 768, 2048], P('pipe', 'dp')
- grad_out: float32 [16, 512, 768], P('pipe', None, 'dp')
The draws below stay inside these ranges and needn't reach their ends.
Inputs may be any that keep to these rules, and one draw needn't show every extreme that they name: `lens_fwd`: each row of 4 lengths sums to 128; its largest is exactly 64. `lens_bwd`: each row of 4 lengths sums to 128; its largest is exactly 64.
All inputs are finite; a program needn't handle non-finite values.
Results may differ from the reference program's by a relative error of at most 0.011.
Values may be sent and summed in bfloat16 or wider, within the bound.
No kernel may reach another device: no remote copies, remote signals or barrier semaphores. Data moves between devices by JAX's collectives and lax.ppermute only.
A program may use at most 32 MiB of HBM per device.

```python
import math
import jax
import jax.numpy as jnp
import numpy as np
from jax import lax

D = 768
HEADS = 4
HEAD_DIM = 128
HID = 512
TOK_DEV = 128
USERS = 4
LMAX = 64
TOKENS = 6144
N_DP = 48
N_PIPE = 16


def with_spikes(array, key, source, target, blocks, factor):
    def block_of(position):
        return (jnp.arange(array.shape[position]) // (array.shape[position] // blocks)).reshape((-1,) + (1,) * (array.ndim - 1 - position))

    first = jax.random.permutation(key, blocks)[block_of(target)]
    far = (block_of(target) + blocks // 2) % blocks
    return jnp.where((block_of(source) == first) | (block_of(source) == far), factor * array, array)


def levels(key, shape, shards, smallest, top_value):
    factor_of = 1.0
    for dim, shards_of in shards:
        steps = jax.random.uniform(jax.random.fold_in(jax.random.fold_in(key, 6), dim), (shards_of,), jnp.float32, smallest / len(shards), top_value / len(shards))
        factor_of = factor_of * jnp.repeat(jnp.exp(steps), shape[dim] // shards_of).reshape((-1,) + (1,) * (len(shape) - 1 - dim))
    return factor_of


def profile(count, total, bound, slope):
    portions = [(1 << 20) // math.isqrt(standing ** slope) + 1 for standing in range(2, count + 1)]
    rest, counts = total - bound - (count - 1), [1] * (count - 1)
    while rest > 0:
        free = [i for i in range(count - 1) if counts[i] < bound]
        whole, budget = sum([portions[i] for i in free]), rest
        for i in free:
            more = min(bound - counts[i], max(1, budget * portions[i] // whole), rest)
            counts[i] = counts[i] + more
            rest = rest - more
    return np.array([bound] + counts)


def uneven_parts(rng, amount, total, limit, slope):
    if amount == 2:
        one = jax.random.randint(rng, (), max(1, total - limit), min(limit, total - 1) + 1)
        return jnp.stack([one, total - one])
    sizes = jnp.asarray(profile(amount, total, limit, slope), jnp.int32)
    twos = (amount - 1) // 2
    giver, taker = sizes[1:1 + 2 * twos:2], sizes[2:2 + 2 * twos:2]
    room = jnp.minimum(giver - 1, limit - taker)
    moved = jax.random.randint(jax.random.fold_in(rng, 1), (twos,), 0, 1 << 20) % (room + 1)
    sizes = sizes.at[1:1 + 2 * twos:2].set(giver - moved).at[2:2 + 2 * twos:2].set(taker + moved)
    return sizes[jax.random.permutation(jax.random.fold_in(rng, 2), amount)]


def noise(rng, shape, scale, most, cuts=(), held_as=jnp.bfloat16):
    values = jax.random.normal(rng, shape, jnp.float32) * scale
    if len(cuts) > 0:
        values = levels(rng, shape, cuts, -0.22, 0.18) * values
    return jnp.clip(values, min=-most, max=most).astype(held_as)


def bell_draw_with(rng, shape, spread, most, cuts, heavy, kind=jnp.bfloat16):
    array = spread * jax.random.normal(rng, shape, jnp.float32)
    if cuts:
        array = array * levels(rng, shape, cuts, -0.22, 0.18)
    return jnp.clip(with_spikes(array, jax.random.fold_in(rng, 3), *heavy), -most, most).astype(kind)


def setup_inputs(seed: int = 0) -> dict:
    key_list = jax.random.split(jax.random.key(seed), 8)
    acts_fwd = noise(key_list[0], (N_PIPE, TOKENS, D), 1.0, 6.0, ((0, 16), (1, 48)))
    acts_bwd = noise(key_list[1], (N_PIPE, TOKENS, D), 1.0, 6.0, ((0, 16), (1, 48)))
    cotangent = bell_draw_with(key_list[2], (N_PIPE, TOKENS, D), 1.0, 6.0, ((0, 16), (1, 48)), (1, 2, 48, 3.25))
    lens_fwd = jax.vmap(lambda own: uneven_parts(own, USERS, TOK_DEV, LMAX, 2))(jax.random.split(key_list[3], N_PIPE * N_DP)).reshape((N_PIPE, N_DP, USERS)).astype(jnp.int32)
    lens_bwd = jax.vmap(lambda own: uneven_parts(own, USERS, TOK_DEV, LMAX, 2))(jax.random.split(key_list[4], N_PIPE * N_DP)).reshape((N_PIPE, N_DP, USERS)).astype(jnp.int32)
    w_proj = noise(key_list[5], (N_PIPE, D, 4 * HID), D ** -0.5, 0.21875, ((0, 16), (1, 48)), jnp.float32)
    w_out = noise(key_list[6], (N_PIPE, HID, D), HID ** -0.5, 0.25, ((0, 16), (2, 48)), jnp.float32)
    return dict(acts_fwd=acts_fwd, acts_bwd=acts_bwd, cotangent=cotangent, lens_fwd=lens_fwd, lens_bwd=lens_bwd, w_proj=w_proj, w_out=w_out)


EPS = 1e-05

def jagged_mask(lengths, count):
    ends = jnp.cumsum(lengths).astype(jnp.int32)
    positions = jnp.arange(count, dtype=jnp.int32)
    segment = lax.optimization_barrier(jnp.sum((positions[:, None] >= ends[None, :]).astype(jnp.int32), axis=1))
    keep = (segment[:, None] == segment[None, :]) & (positions[:, None] >= positions[None, :])
    return keep.astype(jnp.float32)

def layer_norm(values):
    center = values - lax.optimization_barrier(jnp.mean(values, axis=-1, keepdims=True))
    inverse = lax.rsqrt(lax.optimization_barrier(jnp.mean(center * center, axis=-1, keepdims=True)) + EPS)
    return (center * inverse, inverse)

def norm_back(grad_normed, normed, inverse):
    return inverse * (grad_normed - lax.optimization_barrier(jnp.mean(grad_normed, axis=-1, keepdims=True)) - normed * lax.optimization_barrier(jnp.mean(grad_normed * normed, axis=-1, keepdims=True)))

def silu_slope(values):
    sigma = jax.nn.sigmoid(values)
    return sigma * (1.0 + values * (1.0 - sigma))

def forward_parts(tokens, w_first, keep):
    count = tokens.shape[0]
    tok_float = tokens.astype(jnp.float32)
    normed, inverse = layer_norm(tok_float)
    normed_bf = normed.astype(jnp.bfloat16)
    preact = jnp.dot(normed_bf, w_first, preferred_element_type=jnp.float32)
    hidden = jax.nn.silu(preact).astype(jnp.bfloat16)
    gate_u = hidden[:, :HID]
    values_h = hidden[:, HID:2 * HID].reshape(count, HEADS, HEAD_DIM)
    queries = hidden[:, 2 * HID:3 * HID].reshape(count, HEADS, HEAD_DIM)
    keys_h = hidden[:, 3 * HID:].reshape(count, HEADS, HEAD_DIM)
    scores = jnp.einsum('ihd,jhd->hij', queries.astype(jnp.float32), keys_h.astype(jnp.float32)) * HEAD_DIM ** (-0.5)
    attn = (jax.nn.silu(scores) * keep[None] * (1.0 / LMAX)).astype(jnp.bfloat16)
    mixed = jnp.einsum('hij,jhd->ihd', attn.astype(jnp.float32), values_h.astype(jnp.float32)).reshape(count, HID)
    mixed_n, inverse_o = layer_norm(mixed)
    gated = (mixed_n * gate_u.astype(jnp.float32)).astype(jnp.bfloat16)
    return (tok_float, normed, inverse, normed_bf, preact, gate_u, values_h, queries, keys_h, scores, attn, mixed_n, inverse_o, gated)

def forward(tokens, w_first, w_second, keep):
    parts = forward_parts(tokens, w_first, keep)
    return (parts[0] + jnp.dot(parts[13], w_second, preferred_element_type=jnp.float32)).astype(jnp.bfloat16)

def backward(tokens, cotan, w_first, w_second, keep):
    count = tokens.shape[0]
    tok_float, normed, inverse, normed_bf, preact, gate_u, values_h, queries, keys_h, scores, attn, mixed_n, inverse_o, gated = forward_parts(tokens, w_first, keep)
    grad_y = jnp.dot(cotan, w_second.T, preferred_element_type=jnp.float32)
    grad_u = grad_y * mixed_n
    grad_mn = grad_y * gate_u.astype(jnp.float32)
    grad_mixed = norm_back(grad_mn, mixed_n, inverse_o).astype(jnp.bfloat16).reshape(count, HEADS, HEAD_DIM)
    grad_attn = jnp.einsum('ihd,jhd->hij', grad_mixed.astype(jnp.float32), values_h.astype(jnp.float32))
    grad_vals = jnp.einsum('hij,ihd->jhd', attn.astype(jnp.float32), grad_mixed.astype(jnp.float32))
    grad_scores = (grad_attn * keep[None] * (1.0 / LMAX) * silu_slope(scores) * HEAD_DIM ** (-0.5)).astype(jnp.bfloat16)
    grad_q = jnp.einsum('hij,jhd->ihd', grad_scores.astype(jnp.float32), keys_h.astype(jnp.float32))
    grad_k = jnp.einsum('hij,ihd->jhd', grad_scores.astype(jnp.float32), queries.astype(jnp.float32))
    grad_hidden = jnp.concatenate([grad_u, grad_vals.reshape(count, HID), grad_q.reshape(count, HID), grad_k.reshape(count, HID)], axis=1)
    grad_pre = (grad_hidden * silu_slope(preact)).astype(jnp.bfloat16)
    grad_norm = jnp.dot(grad_pre, w_first.T, preferred_element_type=jnp.float32)
    grad_in = (cotan.astype(jnp.float32) + norm_back(grad_norm, normed, inverse)).astype(jnp.bfloat16)
    return (grad_in, normed_bf, grad_pre, gated)

def reference(acts_fwd, acts_bwd, cotangent, lens_fwd, lens_bwd, w_proj, w_out):
    loss_scale = 1.0 / math.sqrt(N_DP * TOK_DEV)

    def phase(items):
        fwd_rows, bwd_rows, cot_rows, fwd_lens, bwd_lens, proj_master, out_master = items
        w_first = proj_master.astype(jnp.bfloat16)
        w_second = out_master.astype(jnp.bfloat16)

        def block(carry, entry):
            fwd_x, bwd_x, cotan, fwd_len, bwd_len = entry
            result = forward(fwd_x, w_first, w_second, jagged_mask(fwd_len, TOK_DEV))
            grad_in, normed_bf, grad_pre, gated = backward(bwd_x, cotan, w_first, w_second, jagged_mask(bwd_len, TOK_DEV))
            term_proj = jnp.dot(normed_bf.T, grad_pre, preferred_element_type=jnp.float32) * loss_scale
            term_out = jnp.dot(gated.T, cotan, preferred_element_type=jnp.float32) * loss_scale
            return ((carry[0] + term_proj, carry[1] + term_out), (result, grad_in))
        start = (jnp.zeros((D, 4 * HID), jnp.float32), jnp.zeros((HID, D), jnp.float32))
        entries = (fwd_rows.reshape(N_DP, TOK_DEV, D), bwd_rows.reshape(N_DP, TOK_DEV, D), cot_rows.reshape(N_DP, TOK_DEV, D), fwd_lens, bwd_lens)
        sums, stacked = lax.scan(block, start, entries)
        return (stacked[0].reshape(TOKENS, D), stacked[1].reshape(TOKENS, D), sums[0], sums[1])
    outputs, grads_in, grad_proj, grad_out = lax.map(phase, (acts_fwd, acts_bwd, cotangent, lens_fwd, lens_bwd, w_proj, w_out))
    next_acts = jnp.roll(outputs, 1, axis=0)
    prev_grads = jnp.roll(grads_in, -1, axis=0)
    return (next_acts, prev_grads, grad_proj, grad_out)
```

```python
import math

import jax
import jax.numpy as jnp
from jax import lax
from jax.sharding import Mesh
from jax.sharding import PartitionSpec as P

HEADS = 4
HEAD_DIM = 128
HID = 512
LMAX = 64
EPS = 1e-05
Z_HIGH, Z_LOW = 4, 3
QUAD = ("x", "c")
ALONG_Z = ("zh", "zl")
ROWS = 128
BF = jnp.bfloat16
F32 = jnp.float32


def shifted(array, axis, by):
    count = lax.axis_size(axis)
    return lax.ppermute(array, axis, [(i, (i + by) % count) for i in range(count)])


def exchanged(array, axis=QUAD):
    return lax.all_to_all(array, axis, split_axis=0, concat_axis=0, tiled=True)


def after(array, *others):
    return lax.optimization_barrier((array, *others))[0]


def quad_summed(parts):
    xi, ci = lax.axis_index("x"), lax.axis_index("c")
    parts = parts.reshape(2, 2, ROWS, -1)
    arrived = shifted(lax.dynamic_index_in_dim(parts, 1 - xi, 0, False), "x", 1)
    pair = lax.dynamic_index_in_dim(parts, xi, 0, False).astype(F32) + arrived.astype(F32)
    arrived = shifted(lax.dynamic_index_in_dim(pair, 1 - ci, 0, False).astype(BF), "c", 1)
    return lax.dynamic_index_in_dim(pair, ci, 0, False) + arrived.astype(F32)


def jagged_mask(lengths):
    ends = jnp.cumsum(lengths, axis=-1)
    positions = jnp.arange(ROWS, dtype=jnp.int32)
    segment = jnp.sum(
        (positions[None, :, None] >= ends[:, None, :]).astype(jnp.int32), axis=-1
    )
    return (segment[:, :, None] == segment[:, None, :]) & (
        positions[None, :, None] >= positions[None, None, :]
    )


def layer_norm(values):
    center = values - jnp.mean(values, axis=-1, keepdims=True)
    inverse = lax.rsqrt(jnp.mean(center * center, axis=-1, keepdims=True) + EPS)
    return (center * inverse, inverse)


def silu_slope(values):
    sigma = jax.nn.sigmoid(values)
    return sigma * (1.0 + values * (1.0 - sigma))


def head_part(tokens, w_head, keep):
    normed_bf = layer_norm(tokens.astype(F32))[0].astype(BF)
    preact = jnp.dot(normed_bf, w_head, preferred_element_type=F32)
    hidden = jax.nn.silu(preact).astype(BF)
    gate = hidden[:, :HEAD_DIM]
    values = hidden[:, HEAD_DIM : 2 * HEAD_DIM].reshape(HEADS, ROWS, HEAD_DIM)
    queries = hidden[:, 2 * HEAD_DIM : 3 * HEAD_DIM].reshape(HEADS, ROWS, HEAD_DIM)
    keys = hidden[:, 3 * HEAD_DIM :].reshape(HEADS, ROWS, HEAD_DIM)
    scores = jnp.einsum("bid,bjd->bij", queries, keys, preferred_element_type=F32) * HEAD_DIM**-0.5
    attn = jnp.where(keep, jax.nn.silu(scores) * (1.0 / LMAX), 0.0).astype(BF)
    mixed = jnp.einsum("bij,bjd->bid", attn, values, preferred_element_type=F32).reshape(
        HEADS * ROWS, HEAD_DIM
    )
    mean = jnp.mean(mixed, axis=-1)
    center = mixed - mean[:, None]
    spread = jnp.sum(center * center, axis=-1)
    return normed_bf, preact, gate, values, queries, keys, scores, attn, center, mean, spread


def per_device(acts_fwd, acts_bwd, cotangent, lens_fwd, lens_bwd, w_proj, w_out):
    loss_scale = 1.0 / math.sqrt(48 * ROWS)

    mine = jnp.concatenate(
        [
            w_proj[0].reshape(16, 4, HEADS, HEAD_DIM).transpose(2, 0, 1, 3).reshape(HEADS, 16, 512),
            w_out[0].T.reshape(16, HEADS, HEAD_DIM).transpose(1, 0, 2),
        ],
        axis=-1,
    ).astype(BF)
    group = exchanged(mine).reshape(64, 640)
    weights = lax.all_gather(group, ALONG_Z, axis=0, tiled=True)
    w_head = weights[:, :512]
    w_back = weights[:, 512:]

    lens = jnp.stack([lens_fwd[0, 0], lens_bwd[0, 0]]).reshape(1, 8).astype(BF)
    pack = jnp.concatenate(
        [acts_fwd[0], acts_bwd[0], cotangent[0], jnp.pad(lens, ((0, 15), (0, 760)))], axis=0
    )
    by_core = shifted(after(pack, mine), "c", 1)
    late = after(pack, group)
    by_chip = shifted(late, "x", 1)
    by_both = lax.ppermute(late, QUAD, [(i, 3 - i) for i in range(4)])
    xi, ci = lax.axis_index("x"), lax.axis_index("c")
    both = jnp.stack([jnp.stack([pack, by_core]), jnp.stack([by_chip, by_both])])
    both = jnp.where(xi == 0, both, both[::-1])
    both = jnp.where(ci == 0, both, both[:, ::-1])
    blocks = both.reshape(4, 400, 768)
    tok_f = blocks[:, :128].reshape(512, 768)
    tok_b = blocks[:, 128:256].reshape(512, 768)
    cotan = blocks[:, 256:384].reshape(512, 768)
    all_lens = blocks[:, 384, :8].astype(jnp.int32)
    keep_f = jagged_mask(all_lens[:, :4])
    keep_b = jagged_mask(all_lens[:, 4:])

    _, _, gate_f, _, _, _, _, _, center_f, mean_f, spread_f = head_part(tok_f, w_head, keep_f)
    normed_bf, preact, gate, values, queries, keys, scores, attn, center, mean, spread = head_part(
        tok_b, w_head, keep_b
    )
    grad_y = jnp.dot(cotan, w_back, preferred_element_type=F32)
    grad_mn = grad_y * gate.astype(F32)
    sum_g = jnp.sum(grad_mn, axis=-1)
    sum_gc = jnp.sum(grad_mn * center, axis=-1)

    stats = lax.all_gather(
        jnp.stack([mean_f, spread_f, mean, spread, sum_g, sum_gc]), QUAD, axis=0, tiled=False
    )
    whole_f = jnp.mean(stats[:, 0], axis=0)
    var_f = (
        jnp.sum(stats[:, 1], axis=0)
        + HEAD_DIM * jnp.sum((stats[:, 0] - whole_f) ** 2, axis=0)
    ) * (1.0 / HID)
    inverse_f = lax.rsqrt(var_f + EPS)
    whole = jnp.mean(stats[:, 2], axis=0)
    var = (
        jnp.sum(stats[:, 3], axis=0) + HEAD_DIM * jnp.sum((stats[:, 2] - whole) ** 2, axis=0)
    ) * (1.0 / HID)
    inverse_o = lax.rsqrt(var + EPS)
    mean_g = jnp.sum(stats[:, 4], axis=0) * (1.0 / HID)
    mean_gm = (
        inverse_o
        * jnp.sum(stats[:, 5] + (stats[:, 2] - whole) * stats[:, 4], axis=0)
        * (1.0 / HID)
    )

    gated_f = ((center_f + (mean_f - whole_f)[:, None]) * inverse_f[:, None] * gate_f.astype(F32)).astype(BF)
    part_f = lax.dot_general(
        gated_f, w_back, (((1,), (1,)), ((), ())), preferred_element_type=F32
    ).astype(BF)

    mixed_n = (center + (mean - whole)[:, None]) * inverse_o[:, None]
    gated = (mixed_n * gate.astype(F32)).astype(BF)
    grad_u = grad_y * mixed_n
    grad_mixed = (
        (inverse_o[:, None] * (grad_mn - mean_g[:, None] - mixed_n * mean_gm[:, None]))
        .astype(BF)
        .reshape(HEADS, ROWS, HEAD_DIM)
    )
    grad_mixed = after(grad_mixed, part_f)
    grad_attn = jnp.einsum("bid,bjd->bij", grad_mixed, values, preferred_element_type=F32)
    grad_vals = jnp.einsum("bij,bid->bjd", attn, grad_mixed, preferred_element_type=F32)
    grad_scores = jnp.where(
        keep_b, grad_attn * (1.0 / LMAX) * silu_slope(scores) * HEAD_DIM**-0.5, 0.0
    ).astype(BF)
    grad_q = jnp.einsum("bij,bjd->bid", grad_scores, keys, preferred_element_type=F32)
    grad_k = jnp.einsum("bij,bid->bjd", grad_scores, queries, preferred_element_type=F32)
    flat = (HEADS * ROWS, HEAD_DIM)
    grad_hidden = jnp.concatenate(
        [grad_u, grad_vals.reshape(flat), grad_q.reshape(flat), grad_k.reshape(flat)], axis=1
    )
    grad_pre = (grad_hidden * silu_slope(preact)).astype(BF)

    across = (((0,), (0,)), ((), ()))
    term_proj = lax.dot_general(normed_bf, grad_pre, across, preferred_element_type=F32)
    term_out = lax.dot_general(cotan, gated, across, preferred_element_type=F32)
    term = jnp.concatenate([term_proj, term_out], axis=1) * loss_scale
    part_b = lax.dot_general(
        grad_pre, w_head, (((1,), (1,)), ((), ())), preferred_element_type=F32
    ).astype(BF)

    summed_f = quad_summed(part_f)
    result = (acts_fwd[0].astype(F32) + summed_f).astype(BF)

    zl = lax.axis_index("zl")
    term = term.reshape(Z_HIGH, Z_LOW, 64, 640).transpose(1, 0, 2, 3).astype(BF)
    ahead = shifted(lax.dynamic_index_in_dim(term, (zl + 1) % 3, 0, False), ALONG_Z, 1)
    behind = shifted(lax.dynamic_index_in_dim(term, (zl + 2) % 3, 0, False), ALONG_Z, -1)
    near = lax.dynamic_index_in_dim(term, zl, 0, False).astype(F32)
    near = (near + ahead.astype(F32) + behind.astype(F32)).astype(BF)
    far = exchanged(after(near, result), "zh")
    grad_norm = quad_summed(part_b)
    next_acts = shifted(result, "pipe", 1)
    normed, inverse = layer_norm(acts_bwd[0].astype(F32))
    grad_in = (
        cotangent[0].astype(F32)
        + inverse
        * (
            grad_norm
            - jnp.mean(grad_norm, axis=-1, keepdims=True)
            - normed * jnp.mean(grad_norm * normed, axis=-1, keepdims=True)
        )
    ).astype(BF)
    prev_grads = shifted(grad_in, "pipe", -1)
    total = jnp.sum(far.astype(F32), axis=0)
    final = exchanged(after(total.reshape(HEADS, 16, 640), grad_in, next_acts))
    grad_proj = (
        final[:, :, :512].reshape(HEADS, 16, 4, HEAD_DIM).transpose(1, 2, 0, 3).reshape(16, 4 * HID)
    )
    grad_out = final[:, :, 512:].transpose(1, 0, 2).reshape(16, HID).T
    return next_acts[None], prev_grads[None], grad_proj[None], grad_out[None]


def solution(mesh):
    pipe = mesh.shape["pipe"]
    fine = Mesh(
        mesh.devices.reshape(Z_HIGH, Z_LOW, 2, 2, pipe), ("zh", "zl", "x", "c", "pipe")
    )
    dp = ("zh", "zl", "x", "c")
    rows = P("pipe", dp, None)
    return jax.shard_map(
        per_device,
        mesh=fine,
        in_specs=(rows, rows, rows, rows, rows, rows, P("pipe", None, dp)),
        out_specs=(rows, rows, rows, P("pipe", None, dp)),
        check_vma=False,
    )
```

```python
import math

import jax
import jax.numpy as jnp
from jax import lax
from jax.experimental import pallas as pl
from jax.experimental.pallas import tpu as pltpu
from jax.sharding import Mesh
from jax.sharding import PartitionSpec as P


HEADS = 4
HEAD_DIM = 128
HID = 512
LMAX = 64
EPS = 1e-05
Z_HIGH, Z_LOW = 4, 3
QUAD = ("x", "c")
ALONG_Z = ("zh", "zl")
ROWS = 128
BF = jnp.bfloat16
F32 = jnp.float32


def shifted(array, axis, by):
    count = lax.axis_size(axis)
    return lax.ppermute(array, axis, [(i, (i + by) % count) for i in range(count)])


def exchanged(array, axis=QUAD):
    return lax.all_to_all(array, axis, split_axis=0, concat_axis=0, tiled=True)


def after(array, *others):
    return lax.optimization_barrier((array, *others))[0]


def quad_summed(parts):
    parts = parts.reshape(2, 2, 2, ROWS, 768)
    arrived = shifted(parts[:, :, 1], "c", 1)
    pair = parts[:, :, 0].astype(F32) + arrived.astype(F32)
    arrived = shifted(pair[:, 1].astype(BF), "x", 1)
    return pair[:, 0] + arrived.astype(F32)


def layer_norm(values):
    center = values - jnp.mean(values, axis=-1, keepdims=True)
    inverse = lax.rsqrt(jnp.mean(center * center, axis=-1, keepdims=True) + EPS)
    return (center * inverse, inverse)


def contract(left, right, left_dim, right_dim):
    return lax.dot_general(
        left, right, (((left_dim,), (right_dim,)), ((), ())), preferred_element_type=F32
    )


def block(r):
    return slice(r * ROWS, (r + 1) * ROWS)


def jagged_mask(row, first):
    lane = lax.broadcasted_iota(jnp.int32, (1, ROWS), 1)
    i = lax.broadcasted_iota(jnp.int32, (ROWS, ROWS), 0).astype(F32)
    j = lax.broadcasted_iota(jnp.int32, (ROWS, ROWS), 1).astype(F32)
    start = jnp.zeros((ROWS, ROWS), F32)
    for k in range(3):
        inside = (lane >= first) & (lane <= first + k)
        end = jnp.sum(jnp.where(inside, row, 0.0), axis=1, keepdims=True)
        start = jnp.maximum(start, jnp.where(i >= end, end, 0.0))
    return (j >= start) & (j <= i)


def in_columns(columns):
    lane = lax.broadcasted_iota(jnp.int32, (ROWS, ROWS), 1)
    whole = jnp.zeros((ROWS, ROWS), F32)
    for k, column in enumerate(columns):
        whole = jnp.where(lane == k, column, whole)
    return whole.T[:8]


def first_kernel(
    place, own, core, chip, both, weights,
    stats, center_f, gate_f, normed_b, hidden_b, slope_b, attn_b, factor_b, center_b, grad_y,
    normed_f, hidden_f,
):
    sources = (own, core, chip, both)
    w_head = weights[:, :512]
    for r, source in enumerate(sources):
        normed_f[block(r)] = layer_norm(source[:ROWS].astype(F32))[0].astype(BF)
        normed_b[block(r)] = layer_norm(source[ROWS : 2 * ROWS].astype(F32))[0].astype(BF)
    for r in range(4):
        preact = jnp.dot(normed_f[block(r)], w_head, preferred_element_type=F32)
        hidden_f[block(r)] = (preact * jax.nn.sigmoid(preact)).astype(BF)
        preact = jnp.dot(normed_b[block(r)], w_head, preferred_element_type=F32)
        sigma = jax.nn.sigmoid(preact)
        hidden_b[block(r)] = (preact * sigma).astype(BF)
        slope_b[block(r)] = sigma * (1.0 + preact * (1.0 - sigma))
        grad_y[block(r)] = jnp.dot(
            sources[r][2 * ROWS : 3 * ROWS], weights[:, 512:], preferred_element_type=F32
        )
    gate_f[...] = hidden_f[:, :HEAD_DIM]
    for r, source in enumerate(sources):
        row = source[3 * ROWS :, :ROWS].astype(F32)[:1]
        columns = []
        for hidden, center_ref, first in ((hidden_f, center_f, 0), (hidden_b, center_b, 4)):
            values = hidden[block(r), HEAD_DIM : 2 * HEAD_DIM]
            queries = hidden[block(r), 2 * HEAD_DIM : 3 * HEAD_DIM]
            keys = hidden[block(r), 3 * HEAD_DIM :]
            keep = jagged_mask(row, first)
            scores = contract(queries, keys, 1, 1) * HEAD_DIM**-0.5
            sigma = jax.nn.sigmoid(scores)
            attn = jnp.where(keep, scores * sigma * (1.0 / LMAX), 0.0).astype(BF)
            mixed = jnp.dot(attn, values, preferred_element_type=F32)
            mean = jnp.mean(mixed, axis=1, keepdims=True)
            center = mixed - mean
            center_ref[block(r)] = center
            columns += [mean, jnp.sum(center * center, axis=1, keepdims=True)]
            if first:
                attn_b[r] = attn
                factor_b[r] = jnp.where(
                    keep,
                    sigma * (1.0 + scores * (1.0 - sigma)) * (HEAD_DIM**-0.5 / LMAX),
                    0.0,
                )
                grad_mn = grad_y[block(r)] * hidden[block(r), :HEAD_DIM].astype(F32)
                columns += [
                    jnp.sum(grad_mn, axis=1, keepdims=True),
                    jnp.sum(grad_mn * center, axis=1, keepdims=True),
                ]
        stats[place[0] ^ r] = in_columns(columns)


def second_kernel(
    place, stats, own, core, chip, both,
    center_f, gate_f, normed_b, hidden_b, slope_b, attn_b, factor_b, center_b, grad_y,
    term_own, term_up, term_down, gated_f, grad_pre,
    gated_b, term,
):
    own_head = place[0]
    for r in range(4):
        b = own_head ^ r
        mine = stats[own_head, b]
        every = [stats[h, b] for h in range(4)]
        whole = (every[0] + every[1] + every[2] + every[3]) * (1.0 / 4)
        gaps = [one - whole for one in every]
        spread = (gaps[0] ** 2 + gaps[1] ** 2 + gaps[2] ** 2 + gaps[3] ** 2) * HEAD_DIM
        inverse_f = lax.rsqrt((4 * whole[1:2] + spread[0:1]) * (1.0 / HID) + EPS)
        inverse_b = lax.rsqrt((4 * whole[3:4] + spread[2:3]) * (1.0 / HID) + EPS)
        mean_g = 4 * whole[4:5] * (1.0 / HID)
        crossed = 4 * whole[5:6]
        for one, gap in zip(every, gaps):
            crossed = crossed + gap[2:3] * one[4:5]
        mean_gm = inverse_b * crossed * (1.0 / HID)
        lines = [mine[0:1] - whole[0:1], inverse_f, mine[2:3] - whole[2:3], inverse_b, mean_g, mean_gm]
        row = lax.broadcasted_iota(jnp.int32, (ROWS, ROWS), 0)
        table = jnp.zeros((ROWS, ROWS), F32)
        for k, line in enumerate(lines):
            table = jnp.where(row == k, line, table)
        table = table.T
        gap_f, inverse_f, gap_b, inverse_b, mean_g, mean_gm = (table[:, k : k + 1] for k in range(6))

        mixed_n = (center_f[block(r)] + gap_f) * inverse_f
        gated_f[block(r)] = (mixed_n * gate_f[block(r)].astype(F32)).astype(BF)
        gate = hidden_b[block(r), :HEAD_DIM].astype(F32)
        values = hidden_b[block(r), HEAD_DIM : 2 * HEAD_DIM]
        queries = hidden_b[block(r), 2 * HEAD_DIM : 3 * HEAD_DIM]
        keys = hidden_b[block(r), 3 * HEAD_DIM :]
        mixed_n = (center_b[block(r)] + gap_b) * inverse_b
        gated_b[block(r)] = (mixed_n * gate).astype(BF)
        grad = grad_y[block(r)]
        grad_mixed = (inverse_b * (grad * gate - mean_g - mixed_n * mean_gm)).astype(BF)
        grad_vals = contract(attn_b[r], grad_mixed, 0, 0)
        grad_scores = (contract(grad_mixed, values, 1, 1) * factor_b[r]).astype(BF)
        grad_q = jnp.dot(grad_scores, keys, preferred_element_type=F32)
        grad_k = contract(grad_scores, queries, 0, 0)
        for k, part in enumerate((grad * mixed_n, grad_vals, grad_q, grad_k)):
            columns = slice(k * HEAD_DIM, (k + 1) * HEAD_DIM)
            grad_pre[block(r), columns] = (part * slope_b[block(r), columns]).astype(BF)
    loss_scale = 1.0 / math.sqrt(48 * ROWS)
    term[:, :512] = (contract(normed_b[...], grad_pre[...], 0, 0) * loss_scale).astype(BF)
    term_out = sum(
        contract(source[2 * ROWS : 3 * ROWS], gated_b[block(r)], 0, 0)
        for r, source in enumerate((own, core, chip, both))
    )
    term[:, 512:] = (term_out * loss_scale).astype(BF)
    for k, out in enumerate((term_own, term_up, term_down)):
        low = lax.rem(place[1] + k, Z_LOW)
        for high in range(Z_HIGH):
            out[high] = term[pl.ds(pl.multiple_of((high * Z_LOW + low) * 64, 64), 64)]


def called(kernel, shapes, scratch, place, *operands):
    scalar = pl.BlockSpec(memory_space=pltpu.SMEM)
    whole = pl.BlockSpec(memory_space=pltpu.VMEM)
    return pl.pallas_call(
        kernel,
        out_shape=[jax.ShapeDtypeStruct(*shape) for shape in shapes],
        in_specs=[scalar] + [whole] * len(operands),
        out_specs=[whole] * len(shapes),
        scratch_shapes=[pltpu.VMEM(*shape) for shape in scratch],
    )(place, *operands)


def per_device(acts_fwd, acts_bwd, cotangent, lens_fwd, lens_bwd, w_proj, w_out):
    mine = jnp.concatenate(
        [
            w_proj[0].reshape(16, 4, HEADS, HEAD_DIM).transpose(2, 0, 1, 3).reshape(HEADS, 16, 512),
            w_out[0].T.reshape(16, HEADS, HEAD_DIM).transpose(1, 0, 2),
        ],
        axis=-1,
    ).astype(BF)
    group = exchanged(mine).reshape(64, 640)
    weights = lax.all_gather(group, ALONG_Z, axis=0, tiled=True)

    lens = jnp.stack([lens_fwd[0, 0], lens_bwd[0, 0]]).reshape(1, 8).astype(BF)
    pack = jnp.concatenate(
        [acts_fwd[0], acts_bwd[0], cotangent[0], jnp.pad(lens, ((0, 15), (0, 760)))], axis=0
    )
    by_core = shifted(after(pack, mine), "c", 1)
    late = after(pack, group)
    by_chip = shifted(late, "x", 1)
    by_both = lax.ppermute(late, QUAD, [(i, 3 - i) for i in range(4)])
    sources = (pack, by_core, by_chip, by_both)
    place = jnp.stack([lax.axis_index(QUAD), lax.axis_index("zl")]).astype(jnp.int32)

    tall, square = (HEADS * ROWS, HEAD_DIM), (HEADS, ROWS, ROWS)
    stats, *kept = called(
        first_kernel,
        (
            ((HEADS, 8, ROWS), F32),
            (tall, F32),
            (tall, BF),
            ((512, 768), BF),
            ((512, 512), BF),
            ((512, 512), F32),
            (square, BF),
            (square, F32),
            (tall, F32),
            (tall, F32),
        ),
        (((512, 768), BF), ((512, 512), BF)),
        place,
        *sources,
        weights,
    )
    every = lax.all_gather(stats, QUAD, axis=0, tiled=False)
    strided = ((Z_HIGH, 64, 640), BF)
    term_own, term_up, term_down, gated_f, grad_pre = called(
        second_kernel,
        (strided, strided, strided, (tall, BF), ((512, 512), BF)),
        ((tall, BF), ((768, 640), BF)),
        place,
        every,
        *sources,
        *kept,
    )

    ahead = shifted(term_up, ALONG_Z, 1)
    behind = shifted(term_down, ALONG_Z, -1)
    near = (term_own.astype(F32) + ahead.astype(F32) + behind.astype(F32)).astype(BF)
    far = exchanged(near, "zh")

    parts = jnp.stack(
        [
            contract(gated_f, weights[:, 512:], 1, 1).astype(BF),
            contract(grad_pre, weights[:, :512], 1, 1).astype(BF),
        ]
    )
    summed = quad_summed(parts.reshape(2, HEADS, ROWS, 768))
    result = (acts_fwd[0].astype(F32) + summed[0]).astype(BF)
    next_acts = shifted(result, "pipe", 1)
    grad_norm = summed[1]
    normed, inverse = layer_norm(acts_bwd[0].astype(F32))
    grad_in = (
        cotangent[0].astype(F32)
        + inverse
        * (
            grad_norm
            - jnp.mean(grad_norm, axis=-1, keepdims=True)
            - normed * jnp.mean(grad_norm * normed, axis=-1, keepdims=True)
        )
    ).astype(BF)
    prev_grads = shifted(grad_in, "pipe", -1)

    total = jnp.sum(far.astype(F32), axis=0)
    final = exchanged(total.reshape(HEADS, 16, 640))
    grad_proj = (
        final[:, :, :512].reshape(HEADS, 16, 4, HEAD_DIM).transpose(1, 2, 0, 3).reshape(16, 4 * HID)
    )
    grad_out = final[:, :, 512:].transpose(1, 0, 2).reshape(16, HID).T
    return next_acts[None], prev_grads[None], grad_proj[None], grad_out[None]


def solution(mesh):
    pipe = mesh.shape["pipe"]
    fine = Mesh(
        mesh.devices.reshape(Z_HIGH, Z_LOW, 2, 2, pipe), ("zh", "zl", "x", "c", "pipe")
    )
    dp = ("zh", "zl", "x", "c")
    rows = P("pipe", dp, None)
    return jax.shard_map(
        per_device,
        mesh=fine,
        in_specs=(rows, rows, rows, rows, rows, rows, P("pipe", None, dp)),
        out_specs=(rows, rows, rows, P("pipe", None, dp)),
        check_vma=False,
    )
```

```python
import math

import jax
import jax.numpy as jnp
from jax import lax
from jax.experimental import pallas as pl
from jax.experimental.pallas import tpu as pltpu
from jax.sharding import Mesh
from jax.sharding import PartitionSpec as P


HEADS = 4
HEAD_DIM = 128
HID = 512
LMAX = 64
EPS = 1e-05
Z_HIGH, Z_LOW = 4, 3
QUAD = ("x", "c")
ALONG_Z = ("zh", "zl")
ROWS = 128
BF = jnp.bfloat16
F32 = jnp.float32


def shifted(array, axis, by):
    count = lax.axis_size(axis)
    return lax.ppermute(array, axis, [(i, (i + by) % count) for i in range(count)])


def exchanged(array, axis=QUAD):
    return lax.all_to_all(array, axis, split_axis=0, concat_axis=0, tiled=True)


def after(array, *others):
    return lax.optimization_barrier((array, *others))[0]


def quad_summed(parts):
    parts = parts.reshape(2, 2, 2, ROWS, 768)
    arrived = shifted(parts[:, :, 1], "c", 1)
    pair = parts[:, :, 0].astype(F32) + arrived.astype(F32)
    arrived = shifted(pair[:, 1].astype(BF), "x", 1)
    return pair[:, 0] + arrived.astype(F32)


def layer_norm(values):
    center = values - jnp.mean(values, axis=-1, keepdims=True)
    inverse = lax.rsqrt(jnp.mean(center * center, axis=-1, keepdims=True) + EPS)
    return (center * inverse, inverse)


def contract(left, right, left_dim, right_dim):
    return lax.dot_general(
        left, right, (((left_dim,), (right_dim,)), ((), ())), preferred_element_type=F32
    )


def block(r):
    return slice(r * ROWS, (r + 1) * ROWS)


def jagged_mask(row, first):
    lane = lax.broadcasted_iota(jnp.int32, (1, ROWS), 1)
    i = lax.broadcasted_iota(jnp.int32, (ROWS, ROWS), 0).astype(F32)
    j = lax.broadcasted_iota(jnp.int32, (ROWS, ROWS), 1).astype(F32)
    start = jnp.zeros((ROWS, ROWS), F32)
    for k in range(3):
        inside = (lane >= first) & (lane <= first + k)
        end = jnp.sum(jnp.where(inside, row, 0.0), axis=1, keepdims=True)
        start = jnp.maximum(start, jnp.where(i >= end, end, 0.0))
    return (j >= start) & (j <= i)


def in_columns(columns):
    lane = lax.broadcasted_iota(jnp.int32, (ROWS, ROWS), 1)
    whole = jnp.zeros((ROWS, ROWS), F32)
    for k, column in enumerate(columns):
        whole = jnp.where(lane == k, column, whole)
    return whole.T[:8]


def weights_kernel(proj, out, mine):
    for h in range(HEADS):
        for k in range(4):
            first = k * HID + h * HEAD_DIM
            mine[h, :, k * HEAD_DIM : (k + 1) * HEAD_DIM] = proj[:, first : first + HEAD_DIM].astype(BF)
        mine[h, :, 512:] = out[:, h * HEAD_DIM : (h + 1) * HEAD_DIM].astype(BF)


def first_kernel(
    place, own, core, chip, both, weights,
    stats, center_f, gate_f, normed_b, hidden_b, slope_b, attn_b, factor_b, center_b, grad_y,
    normed_f, hidden_f,
):
    sources = (own, core, chip, both)
    w_head = weights[:, :512]
    for r, source in enumerate(sources):
        normed_f[block(r)] = layer_norm(source[:ROWS].astype(F32))[0].astype(BF)
        normed_b[block(r)] = layer_norm(source[ROWS : 2 * ROWS].astype(F32))[0].astype(BF)
    for r in range(4):
        preact = jnp.dot(normed_f[block(r)], w_head, preferred_element_type=F32)
        hidden_f[block(r)] = (preact * jax.nn.sigmoid(preact)).astype(BF)
        preact = jnp.dot(normed_b[block(r)], w_head, preferred_element_type=F32)
        sigma = jax.nn.sigmoid(preact)
        hidden_b[block(r)] = (preact * sigma).astype(BF)
        slope_b[block(r)] = sigma * (1.0 + preact * (1.0 - sigma))
        grad_y[block(r)] = jnp.dot(
            sources[r][2 * ROWS : 3 * ROWS], weights[:, 512:], preferred_element_type=F32
        )
    gate_f[...] = hidden_f[:, :HEAD_DIM]
    for r, source in enumerate(sources):
        row = source[3 * ROWS :, :ROWS].astype(F32)[:1]
        columns = []
        for hidden, center_ref, first in ((hidden_f, center_f, 0), (hidden_b, center_b, 4)):
            values = hidden[block(r), HEAD_DIM : 2 * HEAD_DIM]
            queries = hidden[block(r), 2 * HEAD_DIM : 3 * HEAD_DIM]
            keys = hidden[block(r), 3 * HEAD_DIM :]
            keep = jagged_mask(row, first)
            scores = contract(queries, keys, 1, 1) * HEAD_DIM**-0.5
            sigma = jax.nn.sigmoid(scores)
            attn = jnp.where(keep, scores * sigma * (1.0 / LMAX), 0.0).astype(BF)
            mixed = jnp.dot(attn, values, preferred_element_type=F32)
            mean = jnp.mean(mixed, axis=1, keepdims=True)
            center = mixed - mean
            center_ref[block(r)] = center
            columns += [mean, jnp.sum(center * center, axis=1, keepdims=True)]
            if first:
                attn_b[r] = attn
                factor_b[r] = jnp.where(
                    keep,
                    sigma * (1.0 + scores * (1.0 - sigma)) * (HEAD_DIM**-0.5 / LMAX),
                    0.0,
                )
                grad_mn = grad_y[block(r)] * hidden[block(r), :HEAD_DIM].astype(F32)
                columns += [
                    jnp.sum(grad_mn, axis=1, keepdims=True),
                    jnp.sum(grad_mn * center, axis=1, keepdims=True),
                ]
        stats[place[0] ^ r] = in_columns(columns)


def second_kernel(
    place, stats, own, core, chip, both,
    center_f, gate_f, normed_b, hidden_b, slope_b, attn_b, factor_b, center_b, grad_y,
    term_own, term_up, term_down, gated_f, grad_pre,
    gated_b, term,
):
    own_head = place[0]
    for r in range(4):
        b = own_head ^ r
        mine = stats[own_head, b]
        every = [stats[h, b] for h in range(4)]
        whole = (every[0] + every[1] + every[2] + every[3]) * (1.0 / 4)
        gaps = [one - whole for one in every]
        spread = (gaps[0] ** 2 + gaps[1] ** 2 + gaps[2] ** 2 + gaps[3] ** 2) * HEAD_DIM
        inverse_f = lax.rsqrt((4 * whole[1:2] + spread[0:1]) * (1.0 / HID) + EPS)
        inverse_b = lax.rsqrt((4 * whole[3:4] + spread[2:3]) * (1.0 / HID) + EPS)
        mean_g = 4 * whole[4:5] * (1.0 / HID)
        crossed = 4 * whole[5:6]
        for one, gap in zip(every, gaps):
            crossed = crossed + gap[2:3] * one[4:5]
        mean_gm = inverse_b * crossed * (1.0 / HID)
        lines = [mine[0:1] - whole[0:1], inverse_f, mine[2:3] - whole[2:3], inverse_b, mean_g, mean_gm]
        row = lax.broadcasted_iota(jnp.int32, (ROWS, ROWS), 0)
        table = jnp.zeros((ROWS, ROWS), F32)
        for k, line in enumerate(lines):
            table = jnp.where(row == k, line, table)
        table = table.T
        gap_f, inverse_f, gap_b, inverse_b, mean_g, mean_gm = (table[:, k : k + 1] for k in range(6))

        mixed_n = (center_f[block(r)] + gap_f) * inverse_f
        gated_f[block(r)] = (mixed_n * gate_f[block(r)].astype(F32)).astype(BF)
        gate = hidden_b[block(r), :HEAD_DIM].astype(F32)
        values = hidden_b[block(r), HEAD_DIM : 2 * HEAD_DIM]
        queries = hidden_b[block(r), 2 * HEAD_DIM : 3 * HEAD_DIM]
        keys = hidden_b[block(r), 3 * HEAD_DIM :]
        mixed_n = (center_b[block(r)] + gap_b) * inverse_b
        gated_b[block(r)] = (mixed_n * gate).astype(BF)
        grad = grad_y[block(r)]
        grad_mixed = (inverse_b * (grad * gate - mean_g - mixed_n * mean_gm)).astype(BF)
        grad_vals = contract(attn_b[r], grad_mixed, 0, 0)
        grad_scores = (contract(grad_mixed, values, 1, 1) * factor_b[r]).astype(BF)
        grad_q = jnp.dot(grad_scores, keys, preferred_element_type=F32)
        grad_k = contract(grad_scores, queries, 0, 0)
        for k, part in enumerate((grad * mixed_n, grad_vals, grad_q, grad_k)):
            columns = slice(k * HEAD_DIM, (k + 1) * HEAD_DIM)
            grad_pre[block(r), columns] = (part * slope_b[block(r), columns]).astype(BF)
    loss_scale = 1.0 / math.sqrt(48 * ROWS)
    term[:, :512] = (contract(normed_b[...], grad_pre[...], 0, 0) * loss_scale).astype(BF)
    term_out = sum(
        contract(source[2 * ROWS : 3 * ROWS], gated_b[block(r)], 0, 0)
        for r, source in enumerate((own, core, chip, both))
    )
    term[:, 512:] = (term_out * loss_scale).astype(BF)
    for k, out in enumerate((term_own, term_up, term_down)):
        low = lax.rem(place[1] + k, Z_LOW)
        for high in range(Z_HIGH):
            out[high] = term[pl.ds(pl.multiple_of((high * Z_LOW + low) * 64, 64), 64)]


def called(kernel, shapes, scratch, place, *operands):
    scalar = pl.BlockSpec(memory_space=pltpu.SMEM)
    whole = pl.BlockSpec(memory_space=pltpu.VMEM)
    return pl.pallas_call(
        kernel,
        out_shape=[jax.ShapeDtypeStruct(*shape) for shape in shapes],
        in_specs=[scalar] + [whole] * len(operands),
        out_specs=[whole] * len(shapes),
        scratch_shapes=[pltpu.VMEM(*shape) for shape in scratch],
        compiler_params=pltpu.CompilerParams(vmem_limit_bytes=24 << 20),
    )(place, *operands)


def per_device(acts_fwd, acts_bwd, cotangent, lens_fwd, lens_bwd, w_proj, w_out):
    mine = pl.pallas_call(
        weights_kernel, out_shape=jax.ShapeDtypeStruct((HEADS, 16, 640), BF)
    )(w_proj[0], w_out[0].T)
    group = exchanged(mine).reshape(64, 640)
    weights = lax.all_gather(group, ALONG_Z, axis=0, tiled=True)

    lens = jnp.stack([lens_fwd[0, 0], lens_bwd[0, 0]]).reshape(1, 8).astype(BF)
    pack = jnp.concatenate(
        [acts_fwd[0], acts_bwd[0], cotangent[0], jnp.pad(lens, ((0, 15), (0, 760)))], axis=0
    )
    by_core = shifted(after(pack, mine), "c", 1)
    late = after(pack, group)
    by_chip = shifted(late, "x", 1)
    by_both = lax.ppermute(late, QUAD, [(i, 3 - i) for i in range(4)])
    sources = (pack, by_core, by_chip, by_both)
    place = jnp.stack([lax.axis_index(QUAD), lax.axis_index("zl")]).astype(jnp.int32)

    tall, square = (HEADS * ROWS, HEAD_DIM), (HEADS, ROWS, ROWS)
    stats, *kept = called(
        first_kernel,
        (
            ((HEADS, 8, ROWS), F32),
            (tall, F32),
            (tall, BF),
            ((512, 768), BF),
            ((512, 512), BF),
            ((512, 512), F32),
            (square, BF),
            (square, F32),
            (tall, F32),
            (tall, F32),
        ),
        (((512, 768), BF), ((512, 512), BF)),
        place,
        *sources,
        weights,
    )
    every = lax.all_gather(stats, QUAD, axis=0, tiled=False)
    strided = ((Z_HIGH, 64, 640), BF)
    term_own, term_up, term_down, gated_f, grad_pre = called(
        second_kernel,
        (strided, strided, strided, (tall, BF), ((512, 512), BF)),
        ((tall, BF), ((768, 640), BF)),
        place,
        every,
        *sources,
        *kept,
    )

    ahead = shifted(term_up, ALONG_Z, 1)
    behind = shifted(term_down, ALONG_Z, -1)
    near = (term_own.astype(F32) + ahead.astype(F32) + behind.astype(F32)).astype(BF)
    far = exchanged(near, "zh")

    parts = jnp.stack(
        [
            contract(gated_f, weights[:, 512:], 1, 1).astype(BF),
            contract(grad_pre, weights[:, :512], 1, 1).astype(BF),
        ]
    )
    summed = quad_summed(parts.reshape(2, HEADS, ROWS, 768))
    result = (acts_fwd[0].astype(F32) + summed[0]).astype(BF)
    next_acts = shifted(result, "pipe", 1)
    grad_norm = summed[1]
    normed, inverse = layer_norm(acts_bwd[0].astype(F32))
    grad_in = (
        cotangent[0].astype(F32)
        + inverse
        * (
            grad_norm
            - jnp.mean(grad_norm, axis=-1, keepdims=True)
            - normed * jnp.mean(grad_norm * normed, axis=-1, keepdims=True)
        )
    ).astype(BF)
    prev_grads = shifted(grad_in, "pipe", -1)

    total = jnp.sum(far.astype(F32), axis=0)
    final = exchanged(total.reshape(HEADS, 16, 640))
    grad_proj = (
        final[:, :, :512].reshape(HEADS, 16, 4, HEAD_DIM).transpose(1, 2, 0, 3).reshape(16, 4 * HID)
    )
    grad_out = final[:, :, 512:].transpose(1, 0, 2).reshape(16, HID).T
    return next_acts[None], prev_grads[None], grad_proj[None], grad_out[None]


def solution(mesh):
    pipe = mesh.shape["pipe"]
    fine = Mesh(
        mesh.devices.reshape(Z_HIGH, Z_LOW, 2, 2, pipe), ("zh", "zl", "x", "c", "pipe")
    )
    dp = ("zh", "zl", "x", "c")
    rows = P("pipe", dp, None)
    return jax.shard_map(
        per_device,
        mesh=fine,
        in_specs=(rows, rows, rows, rows, rows, rows, P("pipe", None, dp)),
        out_specs=(rows, rows, rows, P("pipe", None, dp)),
        check_vma=False,
    )
```
